256 devices in a mesh: layer: 4 (over x), row: 8 (over y, core), col: 8 (over z).
Axes of the slice: x: 4, y: 4, z: 8, core: 2. Of those that a mesh axis runs over, the one named last changes fastest.
Arguments:
- cols: int32 [512, 16], P(('row', 'col'), 'layer'), may hold values from -1 to 511, as said below
- vals: bfloat16 [512, 16, 256, 256], P(('row', 'col'), 'layer'), as said below
- outcols: int32 [512, 4], P(('row', 'col')), may hold values from -1 to 511, as said below
Outputs:
- purified: bfloat16 [512, 4, 256, 256], P(('row', 'col'), 'layer')
The draws below stay inside these ranges and needn't reach their ends.
Inputs may be any that keep to these rules, and one draw needn't show every extreme that they name: `cols`: slots 4 * l to 4 * l + 3 of block row i hold distinct block columns k with k mod 4 = l and |k - i| <= 6, or -1. Column i is always listed in row i, and k is listed in row i exactly when i is listed in row k. vals[i, s] is block (i, cols[i, s]) of a symmetric matrix: the block listed at (k, i) is the transpose of the one at (i, k). Slots holding -1 hold zeros. `outcols`: block row i lists distinct block columns j with i <= j <= i + 12, always i itself, or -1.
All inputs are finite; a program needn't handle non-finite values.
Results may differ from the reference program's by a relative error of at most 0.0085.
Values may be sent and summed in bfloat16 or wider, within the bound.
No kernel may reach another device: no remote copies, remote signals or barrier semaphores. Data moves between devices by JAX's collectives and lax.ppermute only.
A program may use at most 64 MiB of HBM per device.

```python
import jax
import jax.numpy as jnp
from jax import lax

B = 256
W = 6
KL = 4
KO = 4
GROUPS = 4
NB = 512


def make_cols(key):
    base_key = jax.random.fold_in(key, 11)
    first_key, second_key = jax.random.split(base_key)
    regions = (NB + 7) // 8
    region = jnp.arange(NB) // 8
    limits = jax.random.randint(first_key, (regions,), 35, 100)[region]
    rolls = jax.random.randint(second_key, (NB, W), 0, 100)
    index = jnp.arange(NB)[:, None]
    offsets = jnp.arange(1, W + 1)[None, :]
    upper = (rolls < limits[:, None]) & (index + offsets < NB)
    source = jnp.clip(index - offsets, 0, NB - 1)
    lower = upper[source, offsets - 1] & (index - offsets >= 0)
    table = jnp.concatenate([lower[:, ::-1], jnp.ones((NB, 1), dtype=bool), upper], axis=1)
    group = jnp.arange(GROUPS)[None, :, None]
    step = jnp.arange(KL)[None, None, :]
    rowid = jnp.arange(NB)[:, None, None]
    start = rowid - W + jnp.mod(group - (rowid - W), GROUPS)
    column = start + step * GROUPS
    offset = column - rowid
    inside = (offset <= W) & (column >= 0) & (column < NB)
    listed = jnp.take_along_axis(table, jnp.clip(offset + W, 0, 2 * W).reshape(NB, -1), axis=1).reshape(NB, GROUPS, KL)
    chosen = jnp.where(inside & listed, column, -1)
    return chosen.reshape(NB, GROUPS * KL).astype(jnp.int32)


def block_value(key, first, distance):
    block_key = jax.random.fold_in(jax.random.fold_in(jax.random.fold_in(key, 41), first), distance)
    raw = jax.random.normal(block_key, (B, B), jnp.float32)
    raw = 0.1 * raw
    return jnp.where(distance == 0, 0.70710678 * (raw + raw.T), raw)


def draw_cols(key, part):
    return make_cols(key)


def draw_vals(key, part):
    listing = make_cols(key)

    def one_row(index):
        columns = listing[index]
        first = jnp.minimum(index, columns)
        distance = jnp.abs(columns - index)
        blocks = jax.vmap(lambda a, d: block_value(key, a, d))(jnp.clip(first, 0, NB - 1), distance)
        flipped = jnp.swapaxes(blocks, 1, 2)
        blocks = jnp.where((columns < index)[:, None, None], flipped, blocks)
        blocks = jnp.where((columns >= 0)[:, None, None], blocks, jnp.float32(0.0))
        return blocks.astype(jnp.bfloat16)
    return lax.map(one_row, jnp.arange(NB, dtype=jnp.int32))


def draw_outcols(key, part):
    score_key = jax.random.fold_in(key, 53)
    width = 2 * W + 1
    scores = jax.random.randint(score_key, (NB, width), 0, 1000) * 32 + jnp.arange(width)[None, :]
    scores = scores + jnp.where(jnp.arange(width)[None, :] == 0, 1000000, 0)
    rowid = jnp.arange(NB)[:, None]
    scores = jnp.where(rowid + jnp.arange(width)[None, :] < NB, scores, -1)
    best, picked = lax.top_k(scores, KO)
    return jnp.where(best >= 0, rowid + picked, -1).astype(jnp.int32)


def setup_inputs(seed: int = 0) -> dict:
    arg_keys = jax.random.split(jax.random.key(seed), 4)
    return {
        "cols": draw_cols(jax.random.fold_in(arg_keys[3], 71), 0),
        "vals": draw_vals(jax.random.fold_in(arg_keys[3], 71), 0),
        "outcols": draw_outcols(jax.random.fold_in(arg_keys[3], 71), 0),
    }


def reference(cols, vals, outcols):
    nrows = vals.shape[0]
    groups = cols.shape[1] // KL

    def one_row(index):
        left = vals[index].astype(jnp.float32).reshape(groups, KL, B, B)
        left_cols = cols[index].reshape(groups, KL)
        targets = outcols[index]
        where = jnp.clip(targets, 0, nrows - 1).astype(jnp.int32)
        right = vals[where].astype(jnp.float32).reshape(KO, groups, KL, B, B)
        right_cols = cols[where].reshape(KO, groups, KL)
        hits = ((left_cols[None, :, :, None] == right_cols[:, :, None, :]) & (left_cols[None, :, :, None] >= 0)).astype(jnp.float32)
        moved = jnp.einsum('ogst,ogtab->ogsab', hits, right)
        product = jnp.einsum('gsab,ogscb->ogac', left, moved)
        owned = (left_cols[None, :, :] == targets[:, None, None]).astype(jnp.float32)
        twice = 2.0 * jnp.einsum('ogs,gsab->ogab', owned, left)
        rounded = lax.optimization_barrier((twice - product).astype(jnp.bfloat16))
        total = jnp.sum(rounded.astype(jnp.float32), axis=1)
        total = jnp.where(targets[:, None, None] >= 0, total, jnp.float32(0.0))
        return total.astype(jnp.bfloat16)

    return lax.map(one_row, jnp.arange(nrows, dtype=jnp.int32))
```

```python
import functools

import jax
import jax.numpy as jnp
from jax import lax
from jax.experimental import pallas as pl
from jax.experimental.pallas import tpu as pltpu
from jax.sharding import PartitionSpec as P

ROWS = ("row", "col")
B = 256
BF = jnp.bfloat16
F32 = jnp.float32
SM = pl.BlockSpec(memory_space=pltpu.SMEM)
VM = pl.BlockSpec(memory_space=pltpu.VMEM)
ANY = pl.BlockSpec(memory_space=pl.ANY)

OWN, A1, A2, B1, B2 = 0, 32, 39, 45, 53
TWICE, LEFT, LAYER = 128, 160, 176


def shifted(value, axis, by, wrap=True):
    n = lax.axis_size(axis)
    pairs = [(i, (i + by) % n) for i in range(n) if wrap or 0 <= i + by < n]
    return lax.ppermute(value, axis, pairs)


def first_col(row, layer):
    return row - 6 + ((layer - row + 6) & 3)


def b_first(layer):
    return jnp.where(layer < 2, layer + 4, layer)


def pack_kernel(items, place, cols_t, vals, *rest):
    outs, sems = rest[:-1], rest[-1]
    layer = place[0]
    base = place[1]
    copies = []
    for kind, out, pos, where in items:
        if kind == "a":
            m, t = where
            if t == 3:
                m = (layer + 2) & 3
            row = 4 + m
            col = first_col(row, layer) + 4 * t
        else:
            k1 = b_first(layer)
            low = where < k1 - 1
            row = jnp.where(low, where, jnp.minimum(where - (k1 - 1), k1 + 2))
            col = jnp.where(low, k1, k1 + 4) - 8
        hit = jnp.int32(-1)
        empty = jnp.int32(0)
        for s in range(4):
            c = cols_t[s, row]
            hit = jnp.where(c == base + col, s, hit)
            empty = jnp.where(c < 0, s, empty)
        slot = jnp.where(hit >= 0, hit, empty)
        copy = pltpu.make_async_copy(vals.at[row, slot], outs[out].at[pos], sems.at[len(copies)])
        copy.start()
        copies.append(copy)
    for copy in copies:
        copy.wait()


def pack(place, cols_t, vals, items, sizes, name):
    return pl.pallas_call(
        functools.partial(pack_kernel, items),
        out_shape=[jax.ShapeDtypeStruct((n, B, B), BF) for n in sizes],
        in_specs=[SM, SM, ANY],
        out_specs=[VM] * len(sizes),
        scratch_shapes=[pltpu.SemaphoreType.DMA((len(items),))],
        cost_estimate=pl.CostEstimate(
            flops=0, bytes_accessed=len(items) * 2 * B * B * 2, transcendentals=0
        ),
        name=name,
    )(place, cols_t, vals)


def tables(layer, base, cols, outcols, outcols_h):
    rows = jnp.arange(8, dtype=jnp.int32) - 4
    out = jnp.concatenate([outcols_h[4:], outcols[:4]])
    listed = out >= 0
    row_base = jnp.where((rows < 0) & (base == 0), 64 * 8, base)[:, None]
    i = rows[:, None]
    j = jnp.clip(out - row_base, i, i + 12)
    left = first_col(i, layer)
    k = left[:, :, None] + 4 * jnp.arange(4, dtype=jnp.int32)
    ok = listed[:, :, None] & (k >= j[:, :, None] - 6) & (k <= i[:, :, None] + 6)
    jj = j[:, :, None]
    t = jnp.clip((k - first_col(jj, layer)) >> 2, 0, 3)
    in_a = jnp.where(t == 3, A1 + 6, jnp.where(jj >= -2, A1, A2) + 3 * ((-jj - 1) & 1) + t)
    k1 = b_first(layer)
    in_b = jnp.clip(B1 + jj - 8 + jnp.where(k == k1, 0, k1 - 1), B1, B2 + 3)
    slots = jnp.arange(32, dtype=jnp.int32)
    flat = cols.reshape(32)

    def own(row, col):
        here = (slots >> 2) == row[..., None]
        hit = here & (flat == col[..., None] + base)
        free = here & (flat < 0)
        best = jnp.max(jnp.where(hit, slots + 64, jnp.where(free, slots, -1)), axis=-1)
        return jnp.clip(best & 63, 0, 31)

    in_own = own(jnp.broadcast_to(jj, k.shape[:1] + (4, 4)), jnp.broadcast_to(k, (8, 4, 4)))
    right = jnp.where(jj < 0, in_a, jnp.where(jj < 8, in_own, in_b))
    right = jnp.where(ok, right, -1)
    twice = jnp.where(
        listed & ((j & 3) == layer) & (j <= i + 6), jnp.clip((j - left) >> 2, 0, 3), -1
    )
    k_own = k[4:, 0]
    lefts = own(jnp.broadcast_to(i[4:], (4, 4)), k_own)
    parts = [right.reshape(128), twice.reshape(32), lefts.reshape(16), layer[None]]
    return jnp.concatenate(parts).astype(jnp.int32)


def product_kernel(chunk, shifts, table, vals, *rest):
    halo = rest[: 2 * chunk]
    n_out = len(shifts)
    outs, (bbuf, sem) = rest[2 * chunk : 2 * chunk + n_out], rest[2 * chunk + n_out :]
    a_parts, b_parts = halo[:chunk], halo[chunk:]
    layer = table[LAYER]

    def table_row(r):
        return jnp.where(r < 2, 3 - r - 2 * (chunk - 1), 2 + r + 2 * (chunk - 1))

    def right(r, s, t):
        o = (layer + shifts[s]) & 3
        return table[(table_row(r) * 4 + o) * 4 + t]

    pieces = [(OWN, 32, vals), (A1, 7, a_parts[0])]
    if chunk == 2:
        pieces += [(A2, 6, a_parts[1])]
    pieces += [(B1, 8, b_parts[0])]
    if chunk == 2:
        pieces += [(B2, 4, b_parts[1])]

    def issue(r, carry):
        for s in range(n_out):
            for t in range(4):
                b = right(r, s, t)
                dst = bbuf.at[r * n_out + s, t]
                dsem = sem.at[r * n_out + s, t]

                @pl.when(b < 0)
                def _():
                    dst[...] = jnp.zeros((B, B), BF)

                for start, size, ref in pieces:

                    @pl.when((b >= start) & (b < start + size))
                    def _():
                        pltpu.make_async_copy(ref.at[b - start], dst, dsem).start()

        return carry

    lax.fori_loop(0, 4, issue, 0)

    def compute(halo_rows, r, carry):
        lefts = []
        for t in range(4):
            if not halo_rows:
                lefts.append(vals[table[LEFT + (r - 2 + 2 * (chunk - 1)) * 4 + t]])
            elif t == 3:
                lefts.append(a_parts[0][6])
            else:
                lefts.append(a_parts[chunk - 1][3 * r + t])
        for s in range(n_out):
            for t in range(4):

                @pl.when(right(r, s, t) >= 0)
                def _():
                    pltpu.make_async_copy(
                        vals.at[0], bbuf.at[r * n_out + s, t], sem.at[r * n_out + s, t]
                    ).wait()

            acc = jnp.zeros((B, B), F32)
            for t in range(4):
                acc += lax.dot_general(
                    lefts[t],
                    bbuf[r * n_out + s, t],
                    (((1,), (1,)), ((), ())),
                    preferred_element_type=F32,
                )
            outs[s][r] = (-acc).astype(outs[s].dtype)
            o = (layer + shifts[s]) & 3
            own_t = table[TWICE + table_row(r) * 4 + o]
            for t in range(4):

                @pl.when(own_t == t)
                def _():
                    outs[s][r] = (2.0 * lefts[t].astype(F32) - acc).astype(outs[s].dtype)

        return carry

    lax.fori_loop(0, 2, functools.partial(compute, True), 0)
    lax.fori_loop(2, 4, functools.partial(compute, False), 0)


def products(table, vals, a_parts, b_parts, shifts, dtypes, name):
    n, n_out = 4, len(shifts)
    big = (vals, *a_parts, *b_parts)
    return pl.pallas_call(
        functools.partial(product_kernel, len(a_parts), shifts),
        out_shape=[jax.ShapeDtypeStruct((n, B, B), d) for d in dtypes],
        in_specs=[SM] + [VM] * len(big),
        out_specs=[VM] * n_out,
        scratch_shapes=[
            pltpu.VMEM((n * n_out, 4, B, B), BF),
            pltpu.SemaphoreType.DMA((n * n_out, 4)),
        ],
        compiler_params=pltpu.CompilerParams(vmem_limit_bytes=24 << 20),
        cost_estimate=pl.CostEstimate(
            flops=2 * 4 * n * n_out * B**3,
            bytes_accessed=n * n_out * 8 * B * B * 2,
            transcendentals=0,
        ),
        name=name,
    )(table, *big)


def added(whole, part, first):
    half = whole.shape[0] // 2
    a, b = whole[:half], whole[half:]
    if first:
        a = (a.astype(F32) + part.astype(F32)).astype(BF)
    else:
        b = (b.astype(F32) + part.astype(F32)).astype(BF)
    return jnp.concatenate([a, b])


def per_device(cols, vals, outcols):
    base = (lax.axis_index(ROWS) * 8).astype(jnp.int32)
    layer = lax.axis_index("layer").astype(jnp.int32)
    place = jnp.stack([layer, base])
    cols_t = cols.T
    first = [("a", 0, p, (3, p)) for p in range(3)]
    first += [("a", 0, 3 + p, (2, p)) for p in range(3)] + [("a", 0, 6, (0, 3))]
    first += [("b", 1, p, p) for p in range(8)]
    second = [("a", 2, p, (1, p)) for p in range(3)] + [("a", 2, 3 + p, (0, p)) for p in range(3)]
    second += [("b", 3, p, 8 + p) for p in range(4)]
    outcols_h = shifted(outcols, ROWS, 1)
    a1, b1, a2, b2 = pack(place, cols_t, vals, first + second, (7, 8, 6, 4), "pack")
    b1 = shifted(b1, ROWS, -1, False)
    a1 = shifted(a1, ROWS, 1)
    b2 = shifted(b2, ROWS, -1, False)
    a2 = shifted(a2, ROWS, 1)
    table = tables(layer, base, cols, outcols, outcols_h)
    flat = vals.reshape(32, B, B)

    def far(table, a, b, tag):
        (out,) = products(table, flat, a, b, (2,), (BF,), "far" + tag)
        return shifted(out[:2], "layer", 1), shifted(out[2:], "layer", -1)

    def near(table, a, b, tag):
        return products(table, flat, a, b, (1, 3, 0), (BF, BF, F32), "near" + tag)

    got1 = far(table, (a1,), (b1,), "1")
    up1, down1, own1 = near(table, (a1,), (b1,), "1")
    up1, down1 = added(up1, got1[0], True), added(down1, got1[1], False)
    table2, up1, down1 = lax.optimization_barrier((table, up1, down1))
    up1, down1 = shifted(up1, "layer", 1), shifted(down1, "layer", -1)
    got2 = far(table2, (a1, a2), (b1, b2), "2")
    up2, down2, own2 = near(table2, (a1, a2), (b1, b2), "2")
    one = (own1 + up1.astype(F32) + down1.astype(F32)).astype(BF)
    sent1 = shifted(one[:2], ROWS, -1)
    up2, down2 = added(up2, got2[0], True), added(down2, got2[1], False)
    up2, down2 = shifted(up2, "layer", 1), shifted(down2, "layer", -1)
    two = (own2 + up2.astype(F32) + down2.astype(F32)).astype(BF)
    sent2 = shifted(two[:2], ROWS, -1)
    mine = jnp.concatenate([one[2:], two[2:], sent2[::-1], sent1[::-1]])
    return mine[:, None]


def solution(mesh):
    in_specs = (
        P(ROWS, "layer"),
        P(ROWS, "layer", None, None),
        P(ROWS, None),
    )
    out_specs = P(ROWS, "layer", None, None)
    return jax.shard_map(
        per_device, mesh=mesh, in_specs=in_specs, out_specs=out_specs, check_vma=False
    )
```

```python
import functools

import jax
import jax.numpy as jnp
from jax import lax
from jax.experimental import pallas as pl
from jax.experimental.pallas import tpu as pltpu
from jax.sharding import PartitionSpec as P

ROWS = ("row", "col")
B = 256
BF = jnp.bfloat16
F32 = jnp.float32
I32 = jnp.int32
SM = pl.BlockSpec(memory_space=pltpu.SMEM)
VM = pl.BlockSpec(memory_space=pltpu.VMEM)
ANY = pl.BlockSpec(memory_space=pl.ANY)
HBM = pl.BlockSpec(memory_space=pltpu.HBM)

A_PARTS = (7, 5)
B_PARTS = (7, 4)
A0 = 32
B0 = A0 + sum(A_PARTS)
TURN = B0 + sum(B_PARTS)
ZERO = TURN + 2
POOL = ZERO + 1
TWICE, LEFT, OWN, ENTRIES = 64, 80, 112, 144


def shifted(value, axis, by, wrap=True):
    n = lax.axis_size(axis)
    pairs = [(i, (i + by) % n) for i in range(n) if wrap or 0 <= i + by < n]
    return lax.ppermute(value, axis, pairs)


def in_hbm(value):
    return pltpu.with_memory_space_constraint(value, pltpu.HBM)


def here():
    layer = lax.axis_index("layer").astype(I32)
    device = lax.axis_index(ROWS).astype(I32)
    return layer, device


def first_col(row, layer):
    return row - 6 + ((layer - row + 6) & 3)


def b_first(layer):
    return jnp.where(layer < 2, layer + 4, layer)


def a_count(m, layer):
    return 3 + jnp.where(m == ((layer + 2) & 3), 1, 0) - jnp.where(m == layer, 1, 0)


def a_start(m, layer):
    start = jnp.int32(0)
    for above in (3, 2, 1):
        start += jnp.where(m < above, a_count(above, layer), 0)
    return start


def b_turned(layer):
    return layer + jnp.where(layer < 2, 0, b_first(layer) - 1)


def slot_of(cols_t, row, col):
    hit = jnp.int32(-1)
    empty = jnp.int32(0)
    for s in range(4):
        c = cols_t[s, row]
        hit = jnp.where(c == col, s, hit)
        empty = jnp.where(c < 0, s, empty)
    return jnp.where(hit >= 0, hit, empty)


def pack_kernel(cols_hbm, outcols_hbm, vals, *rest):
    outs, (cols_t, outcols_t, sems, ints_sem) = rest[:4], rest[4:]
    ints = [
        pltpu.make_async_copy(cols_hbm, cols_t, ints_sem.at[0]),
        pltpu.make_async_copy(outcols_hbm, outcols_t, ints_sem.at[1]),
    ]
    for copy in ints:
        copy.start()
    for copy in ints:
        copy.wait()
    layer, device = here()
    base = device * 8
    copies = []

    def send(row, col, dst):
        slot = slot_of(cols_t, row, base + col)
        copy = pltpu.make_async_copy(vals.at[row, slot], dst, sems.at[len(copies)])
        copy.start()
        copies.append(copy)

    def a_block(p):
        m = jnp.int32(3)
        t = jnp.int32(p)
        for above in (3, 2, 1):
            past = p >= a_start(above - 1, layer)
            m = jnp.where(past, above - 1, m)
        t = p - a_start(m, layer)
        row = 4 + m
        return row, first_col(row, layer) + 4 * t

    def b_block(p):
        q = p + jnp.where(p >= b_turned(layer), 1, 0)
        k1 = b_first(layer)
        low = q < k1 - 1
        d = jnp.where(low, q, jnp.minimum(q - (k1 - 1), k1 + 2))
        return d, jnp.where(low, k1, k1 + 4) - 8

    p_a = p_b = 0
    for part in range(2):
        for p in range(A_PARTS[part]):
            dst = outs[0].at[pl.ds(p * B, B)] if part == 0 else outs[2].at[p]
            send(*a_block(p_a), dst)
            p_a += 1
        for p in range(B_PARTS[part]):
            send(*b_block(p_b), outs[2 * part + 1].at[p])
            p_b += 1
    line = lax.broadcasted_iota(I32, (16, B), 0)
    listing = jnp.zeros((16, B), F32)
    for m in range(4):
        for o in range(4):
            col = outcols_t[o, 4 + m]
            away = jnp.where(col >= 0, col - base - 4 - m, -1).astype(F32)
            listing = jnp.where(line == m * 4 + o, away, listing)
    outs[0][pl.ds(A_PARTS[0] * B, 16)] = listing.astype(BF)
    for copy in copies:
        copy.wait()


NOTHING = pl.CostEstimate(flops=0, bytes_accessed=0, transcendentals=0)


def pack(cols_t, outcols_t, vals):
    sizes = (A_PARTS[0], B_PARTS[0], A_PARTS[1], B_PARTS[1])
    shapes = [(A_PARTS[0] * B + 16, B)] + [(n, B, B) for n in sizes[1:]]
    return pl.pallas_call(
        pack_kernel,
        out_shape=[jax.ShapeDtypeStruct(shape, BF) for shape in shapes],
        in_specs=[HBM, HBM, HBM],
        out_specs=[VM] * 4,
        scratch_shapes=[
            pltpu.SMEM((4, 8), I32),
            pltpu.SMEM((4, 8), I32),
            pltpu.SemaphoreType.DMA((sum(sizes),)),
            pltpu.SemaphoreType.DMA((2,)),
        ],
        compiler_params=pltpu.CompilerParams(vmem_limit_bytes=4 << 20),
        cost_estimate=NOTHING,
        name="pack",
    )(in_hbm(cols_t), in_hbm(outcols_t), in_hbm(vals))


def left_place(i, t, layer):
    m = i + 4
    place = jnp.where((m == layer) & (t == 2), TURN, A0 + a_start(m, layer) + t)
    return jnp.where(first_col(i, layer) + 4 * t <= i + 6, place, ZERO)


def row_entries(i, away, layer, table, left, right, twice, at):
    first = first_col(i, layer)
    listed = away >= 0
    j = i + jnp.clip(away, 0, 12)
    first_j = first_col(j, layer)
    start_j = A0 + a_start(j + 4, layer)
    k1 = b_first(layer)
    gap = b_turned(layer)
    for t in range(4):
        k = first + 4 * t
        t_j = jnp.clip((k - first_j) >> 2, 0, 3)
        in_a = jnp.where((j + 4 == layer) & (t_j == 2), TURN, start_j + t_j)
        pos = j - 8 + jnp.where(k == k1, 0, k1 - 1)
        in_b = jnp.where(pos == gap, TURN + 1, B0 + pos - jnp.where(pos > gap, 1, 0))
        place = jnp.where(j < 0, in_a, table[OWN + jnp.clip(j, 0, 7) * 4 + t_j])
        place = jnp.clip(jnp.where(j < 8, place, in_b), 0, ZERO)
        ok = listed & (k >= j - 6) & (k <= i + 6)
        right[at * 4 + t] = jnp.where(ok, place, ZERO)
    doubled = listed & ((j & 3) == layer) & (j <= i + 6)
    t_i = jnp.clip((j - first) >> 2, 0, 3)
    twice(at, jnp.where(doubled, left(t_i), ZERO))


def prepare_kernel(cols_t, outcols_t, vals, table, pool, blocks, sem):
    layer, device = here()
    base = device * 8
    copies = [pltpu.make_async_copy(vals.reshape(32, B, B), pool.at[:A0], sem.at[2])]
    for x, (row, col) in enumerate(((layer, layer - 4), (4 + layer, 8 + layer))):
        slot = slot_of(cols_t, row, base + col)
        copies.append(pltpu.make_async_copy(vals.at[row, slot], blocks.at[x], sem.at[x]))
    for copy in copies:
        copy.start()
    pool[ZERO] = jnp.zeros((B, B), BF)

    def own_row(row, carry):
        first = first_col(row, layer)
        for t in range(4):
            place = row * 4 + slot_of(cols_t, row, base + first + 4 * t)
            table[OWN + row * 4 + t] = place
            valid = first + 4 * t <= row + 6

            @pl.when(row < 4)
            def _():
                table[LEFT + 16 + row * 4 + t] = jnp.where(valid, place, ZERO)
                table[LEFT + row * 4 + t] = left_place(row - 4, jnp.int32(t), layer)

        return carry

    lax.fori_loop(0, 8, own_row, 0)

    def one_row(i, carry):
        def left(t):
            return table[LEFT + 16 + i * 4 + t]

        def twice(at, value):
            table[TWICE + at] = value

        for o in range(4):
            col = outcols_t[o, i]
            away = jnp.where(col >= 0, col - base - i, -1)
            row_entries(i, away, layer, table, left, table, twice, i * 4 + o)
        return carry

    lax.fori_loop(0, 4, one_row, 0)
    for copy in copies:
        copy.wait()
    for x in range(2):
        pool[TURN + x] = blocks[x].T


def prepare(cols_t, outcols_t, vals):
    return pl.pallas_call(
        prepare_kernel,
        out_shape=[
            jax.ShapeDtypeStruct((ENTRIES,), I32),
            jax.ShapeDtypeStruct((POOL, B, B), BF),
        ],
        in_specs=[SM, SM, HBM],
        out_specs=[SM, VM],
        scratch_shapes=[pltpu.VMEM((2, B, B), BF), pltpu.SemaphoreType.DMA((3,))],
        compiler_params=pltpu.CompilerParams(vmem_limit_bytes=4 << 20),
        cost_estimate=NOTHING,
        name="prepare",
    )(cols_t, outcols_t, in_hbm(vals))


TARGETS = {(2, 0): (0, 0), (1, 1): (0, 2), (2, 1): (1, 0), (3, 0): (1, 2)}
TARGETS |= {(1, 0): (2, 0), (3, 1): (3, 0), (0, 0): (4, 0), (0, 1): (5, 0)}
SIZES = (4, 4, 2, 2, 2, 2)


def product_kernel(chunk, table, pool_in, listing, b_part, *rest):
    a_parts, rest = rest[: chunk - 1], rest[chunk - 1 :]
    outs, (pool, lines, away, right, twice, sem) = rest[:6], rest[6:]
    layer, _ = here()
    first_rows = A_PARTS[0] * B
    listed = pltpu.make_async_copy(listing.at[pl.ds(first_rows, 16)], lines, sem.at[0])
    listed.start()
    start = B0 + sum(B_PARTS[: chunk - 1])
    pieces = [(b_part, start, B_PARTS[chunk - 1])]
    if chunk == 1:
        pieces += [(listing.at[pl.ds(p * B, B)], A0 + p, 0) for p in range(A_PARTS[0])]
    else:
        pieces += [(a_parts[0], A0 + A_PARTS[0], A_PARTS[1])]
    copies = [
        pltpu.make_async_copy(
            ref, pool.at[start : start + size] if size else pool.at[start], sem.at[1 + x]
        )
        for x, (ref, start, size) in enumerate(pieces)
    ]
    for copy in copies:
        copy.start()
    listed.wait()
    away[...] = lines[:, :128].astype(F32).astype(I32)

    def row_of(above, r):
        return r + 2 * (chunk - 1) if above else -1 - r - 2 * (chunk - 1)

    def below_row(r, carry):
        i = row_of(0, r)

        def left(t):
            return table[LEFT + (i + 4) * 4 + t]

        def store(at, value):
            twice[at] = value

        for o in range(4):
            far = away[(i + 4) * 4 + o, 0]
            row_entries(i, far, layer, table, left, right, store, r * 4 + o)
        return carry

    lax.fori_loop(0, 2, below_row, 0)
    for copy in copies:
        copy.wait()

    def compute(above, r, carry):
        i = row_of(above, r)
        lefts = [table[LEFT + (i + 4) * 4 + t] for t in range(4)]
        for shift in (2, 1, 3, 0):
            o = (layer + shift) & 3
            acc = jnp.zeros((B, B), F32)
            for t in range(4):
                place = table[(i * 4 + o) * 4 + t] if above else right[(r * 4 + o) * 4 + t]
                acc += lax.dot_general(
                    pool[lefts[t]],
                    pool[place],
                    (((1,), (1,)), ((), ())),
                    preferred_element_type=F32,
                )
            own = table[TWICE + i * 4 + o] if above else twice[r * 4 + o]
            factor = jnp.where(own < ZERO, 2.0, 0.0).astype(F32)
            out, start = TARGETS[shift, above]
            outs[out][start + r] = (factor * pool[own].astype(F32) - acc).astype(BF)
        return carry

    lax.fori_loop(0, 2, functools.partial(compute, 0), 0)
    lax.fori_loop(0, 2, functools.partial(compute, 1), 0)


def products(table, pool, halo, chunk, name):
    return pl.pallas_call(
        functools.partial(product_kernel, chunk),
        out_shape=[jax.ShapeDtypeStruct((n, B, B), BF) for n in (*SIZES, POOL)],
        in_specs=[SM, VM] + [ANY] * len(halo),
        out_specs=[VM] * (len(SIZES) + 1),
        scratch_shapes=[
            pltpu.VMEM((16, B), BF),
            pltpu.VMEM((16, 128), I32),
            pltpu.SMEM((32,), I32),
            pltpu.SMEM((8,), I32),
            pltpu.SemaphoreType.DMA((2 + A_PARTS[0],)),
        ],
        input_output_aliases={1: len(SIZES)},
        compiler_params=pltpu.CompilerParams(vmem_limit_bytes=4 << 20),
        cost_estimate=NOTHING,
        name=name,
    )(table, pool, *halo)


def total(*parts):
    return sum(part.astype(F32) for part in parts).astype(BF)


def adds_kernel(a, b, c, d, x, y):
    x[...] = total(a[...], b[:2])
    y[...] = total(c[...], d[:2])


def adds(a, b, c, d, name, cost):
    return pl.pallas_call(
        adds_kernel,
        out_shape=[jax.ShapeDtypeStruct((2, B, B), BF)] * 2,
        in_specs=[VM] * 4,
        out_specs=[VM] * 2,
        compiler_params=pltpu.CompilerParams(vmem_limit_bytes=4 << 20),
        cost_estimate=pl.CostEstimate(flops=0, bytes_accessed=cost, transcendentals=0),
        name=name,
    )(a, b, c, d)


def finish_kernel(sums, copied, *rest):
    n_in = 3 * len(sums) + len(copied)
    parts, (out, block, sem) = rest[:n_in], rest[-3:]
    copies = []

    def send(src, row):
        copy = pltpu.make_async_copy(src, out.at[row], sem.at[len(copies)])
        copy.start()
        copies.append(copy)

    for x, rows in enumerate(copied):
        for r in range(2):
            send(parts[3 * len(sums) + x].at[r], rows[r])
    for x, rows in enumerate(sums):
        own, plus, minus = parts[3 * x : 3 * x + 3]
        for r in range(2):
            block[2 * x + r] = total(own[r], plus[2 + r], minus[r])
            send(block.at[2 * x + r], rows[r])
    for copy in copies:
        copy.wait()


def finish(sums, copied, parts, before, name):
    n = 2 * len(sums) + 2 * len(copied)
    return pl.pallas_call(
        functools.partial(finish_kernel, sums, copied),
        out_shape=jax.ShapeDtypeStruct((8, B, B), BF),
        in_specs=[VM] * len(parts) + [HBM] * len(before),
        out_specs=HBM,
        scratch_shapes=[
            pltpu.VMEM((max(2 * len(sums), 1), B, B), BF),
            pltpu.SemaphoreType.DMA((n,)),
        ],
        input_output_aliases={len(parts): 0} if before else {},
        compiler_params=pltpu.CompilerParams(vmem_limit_bytes=4 << 20),
        cost_estimate=NOTHING,
        name=name,
    )(*parts, *before)


def per_device(cols, vals, outcols):
    both = lax.optimization_barrier
    a1, b1, a2, b2 = pack(cols.T, outcols.T, vals)
    a1 = shifted(a1, ROWS, 1)
    b1 = shifted(b1, ROWS, -1, False)
    a2 = shifted(a2, ROWS, 1)
    b2 = shifted(b2, ROWS, -1, False)
    table, pool = prepare(cols.T, outcols.T, vals)

    out1 = products(table, pool, (a1, b1), 1, "products1")
    plus1, minus1, up_b1, down1, own_b1, own1, pool = out1
    plus1, minus1 = shifted(plus1, "layer", 1), shifted(minus1, "layer", -1)
    out2 = products(table, pool, (a1, b2, a2), 2, "products2")
    plus2, minus2, up_b2, down2, own_b2, own2, pool = out2
    (plus1, minus1), _ = both(((plus1, minus1), own_b2))
    plus2, minus2 = shifted(plus2, "layer", 1), shifted(minus2, "layer", -1)

    def second(plus, minus, up_below, down, own_below, name, cost):
        up_below, down = adds(up_below, plus, down, minus, name, cost)
        up_below = shifted(up_below, "layer", 1)
        down = shifted(down, "layer", -1)
        below = shifted(total(own_below, minus[2:], up_below), ROWS, -1)
        return down, below

    down1, below1 = second(plus1, minus1, up_b1, down1, own_b1, "adds1", 40 << 20)
    plus2, minus2 = both((plus2, minus2))
    down2, below2 = second(plus2, minus2, up_b2, down2, own_b2, "adds2", 0)
    parts = (own1, plus1, down1, own2, plus2, down2, below1)
    mine = finish(((0, 1), (2, 3)), ((7, 6),), parts, (), "finish1")
    mine = finish((), ((5, 4),), (below2,), (mine,), "finish2")
    return mine[:, None]


def solution(mesh):
    in_specs = (
        P(ROWS, "layer"),
        P(ROWS, "layer", None, None),
        P(ROWS, None),
    )
    out_specs = P(ROWS, "layer", None, None)
    return jax.shard_map(
        per_device, mesh=mesh, in_specs=in_specs, out_specs=out_specs, check_vma=False
    )
```

```python
import functools

import jax
import jax.numpy as jnp
from jax import lax
from jax.experimental import pallas as pl
from jax.experimental.pallas import tpu as pltpu
from jax.sharding import PartitionSpec as P

ROWS = ("row", "col")
B = 256
BF = jnp.bfloat16
F32 = jnp.float32
I32 = jnp.int32
SM = pl.BlockSpec(memory_space=pltpu.SMEM)
VM = pl.BlockSpec(memory_space=pltpu.VMEM)
ANY = pl.BlockSpec(memory_space=pl.ANY)
HBM = pl.BlockSpec(memory_space=pltpu.HBM)

A_PARTS = (7, 5)
B_PARTS = (7, 4)
A0 = 32
B0 = A0 + sum(A_PARTS)
TURN = B0 + sum(B_PARTS)
ZERO = TURN + 2
POOL = ZERO + 1
TWICE, LEFT, OWN, ENTRIES = 64, 80, 112, 144


def shifted(value, axis, by, wrap=True):
    n = lax.axis_size(axis)
    pairs = [(i, (i + by) % n) for i in range(n) if wrap or 0 <= i + by < n]
    return lax.ppermute(value, axis, pairs)


def in_hbm(value):
    return pltpu.with_memory_space_constraint(value, pltpu.HBM)


def here():
    layer = lax.axis_index("layer").astype(I32)
    device = lax.axis_index(ROWS).astype(I32)
    return layer, device


def first_col(row, layer):
    return row - 6 + ((layer - row + 6) & 3)


def b_first(layer):
    return jnp.where(layer < 2, layer + 4, layer)


def a_count(m, layer):
    return 3 + jnp.where(m == ((layer + 2) & 3), 1, 0) - jnp.where(m == layer, 1, 0)


def a_start(m, layer):
    start = jnp.int32(0)
    for above in (3, 2, 1):
        start += jnp.where(m < above, a_count(above, layer), 0)
    return start


def b_turned(layer):
    return layer + jnp.where(layer < 2, 0, b_first(layer) - 1)


def slot_of(cols_t, row, col):
    hit = jnp.int32(-1)
    empty = jnp.int32(0)
    for s in range(4):
        c = cols_t[s, row]
        hit = jnp.where(c == col, s, hit)
        empty = jnp.where(c < 0, s, empty)
    return jnp.where(hit >= 0, hit, empty)


def pack_kernel(cols_hbm, outcols_hbm, vals, *rest):
    outs, (cols_t, outcols_t, sems, ints_sem) = rest[:4], rest[4:]
    ints = [
        pltpu.make_async_copy(cols_hbm, cols_t, ints_sem.at[0]),
        pltpu.make_async_copy(outcols_hbm, outcols_t, ints_sem.at[1]),
    ]
    for copy in ints:
        copy.start()
    for copy in ints:
        copy.wait()
    layer, device = here()
    base = device * 8
    copies = []

    def send(row, col, dst):
        slot = slot_of(cols_t, row, base + col)
        copy = pltpu.make_async_copy(vals.at[row, slot], dst, sems.at[len(copies)])
        copy.start()
        copies.append(copy)

    def a_block(p):
        m = jnp.int32(3)
        t = jnp.int32(p)
        for above in (3, 2, 1):
            past = p >= a_start(above - 1, layer)
            m = jnp.where(past, above - 1, m)
        t = p - a_start(m, layer)
        row = 4 + m
        return row, first_col(row, layer) + 4 * t

    def b_block(p):
        q = p + jnp.where(p >= b_turned(layer), 1, 0)
        k1 = b_first(layer)
        low = q < k1 - 1
        d = jnp.where(low, q, jnp.minimum(q - (k1 - 1), k1 + 2))
        return d, jnp.where(low, k1, k1 + 4) - 8

    p_a = p_b = 0
    for part in range(2):
        for p in range(A_PARTS[part]):
            dst = outs[0].at[pl.ds(p * B, B)] if part == 0 else outs[2].at[p]
            send(*a_block(p_a), dst)
            p_a += 1
        for p in range(B_PARTS[part]):
            send(*b_block(p_b), outs[2 * part + 1].at[p])
            p_b += 1
    line = lax.broadcasted_iota(I32, (16, B), 0)
    listing = jnp.zeros((16, B), F32)
    for m in range(4):
        for o in range(4):
            col = outcols_t[o, 4 + m]
            away = jnp.where(col >= 0, col - base - 4 - m, -1).astype(F32)
            listing = jnp.where(line == m * 4 + o, away, listing)
    outs[0][pl.ds(A_PARTS[0] * B, 16)] = listing.astype(BF)
    for copy in copies:
        copy.wait()


NOTHING = pl.CostEstimate(flops=0, bytes_accessed=0, transcendentals=0)


def pack(cols_t, outcols_t, vals):
    sizes = (A_PARTS[0], B_PARTS[0], A_PARTS[1], B_PARTS[1])
    shapes = [(A_PARTS[0] * B + 16, B)] + [(n, B, B) for n in sizes[1:]]
    return pl.pallas_call(
        pack_kernel,
        out_shape=[jax.ShapeDtypeStruct(shape, BF) for shape in shapes],
        in_specs=[HBM, HBM, HBM],
        out_specs=[VM] * 4,
        scratch_shapes=[
            pltpu.SMEM((4, 8), I32),
            pltpu.SMEM((4, 8), I32),
            pltpu.SemaphoreType.DMA((sum(sizes),)),
            pltpu.SemaphoreType.DMA((2,)),
        ],
        compiler_params=pltpu.CompilerParams(vmem_limit_bytes=4 << 20),
        cost_estimate=NOTHING,
        name="pack",
    )(in_hbm(cols_t), in_hbm(outcols_t), in_hbm(vals))


def left_place(i, t, layer):
    m = i + 4
    place = jnp.where((m == layer) & (t == 2), TURN, A0 + a_start(m, layer) + t)
    return jnp.where(first_col(i, layer) + 4 * t <= i + 6, place, ZERO)


def row_entries(i, away, layer, table, left, right, twice, at):
    first = first_col(i, layer)
    listed = away >= 0
    j = i + jnp.clip(away, 0, 12)
    first_j = first_col(j, layer)
    start_j = A0 + a_start(j + 4, layer)
    k1 = b_first(layer)
    gap = b_turned(layer)
    for t in range(4):
        k = first + 4 * t
        t_j = jnp.clip((k - first_j) >> 2, 0, 3)
        in_a = jnp.where((j + 4 == layer) & (t_j == 2), TURN, start_j + t_j)
        pos = j - 8 + jnp.where(k == k1, 0, k1 - 1)
        in_b = jnp.where(pos == gap, TURN + 1, B0 + pos - jnp.where(pos > gap, 1, 0))
        place = jnp.where(j < 0, in_a, table[OWN + jnp.clip(j, 0, 7) * 4 + t_j])
        place = jnp.clip(jnp.where(j < 8, place, in_b), 0, ZERO)
        ok = listed & (k >= j - 6) & (k <= i + 6)
        right[at * 4 + t] = jnp.where(ok, place, ZERO)
    doubled = listed & ((j & 3) == layer) & (j <= i + 6)
    t_i = jnp.clip((j - first) >> 2, 0, 3)
    twice(at, jnp.where(doubled, left(t_i), ZERO))


def prepare_kernel(cols_t, outcols_t, vals, table, pool, blocks, sem):
    layer, device = here()
    base = device * 8
    copies = [pltpu.make_async_copy(vals.reshape(32, B, B), pool.at[:A0], sem.at[2])]
    for x, (row, col) in enumerate(((layer, layer - 4), (4 + layer, 8 + layer))):
        slot = slot_of(cols_t, row, base + col)
        copies.append(pltpu.make_async_copy(vals.at[row, slot], blocks.at[x], sem.at[x]))
    for copy in copies:
        copy.start()
    pool[ZERO] = jnp.zeros((B, B), BF)

    def own_row(row, carry):
        first = first_col(row, layer)
        for t in range(4):
            place = row * 4 + slot_of(cols_t, row, base + first + 4 * t)
            table[OWN + row * 4 + t] = place
            valid = first + 4 * t <= row + 6

            @pl.when(row < 4)
            def _():
                table[LEFT + 16 + row * 4 + t] = jnp.where(valid, place, ZERO)
                table[LEFT + row * 4 + t] = left_place(row - 4, jnp.int32(t), layer)

        return carry

    lax.fori_loop(0, 8, own_row, 0)

    def one_row(i, carry):
        def left(t):
            return table[LEFT + 16 + i * 4 + t]

        def twice(at, value):
            table[TWICE + at] = value

        for o in range(4):
            col = outcols_t[o, i]
            away = jnp.where(col >= 0, col - base - i, -1)
            row_entries(i, away, layer, table, left, table, twice, i * 4 + o)
        return carry

    lax.fori_loop(0, 4, one_row, 0)
    for copy in copies:
        copy.wait()
    for x in range(2):
        pool[TURN + x] = blocks[x].T


def prepare(cols_t, outcols_t, vals):
    return pl.pallas_call(
        prepare_kernel,
        out_shape=[
            jax.ShapeDtypeStruct((ENTRIES,), I32),
            jax.ShapeDtypeStruct((POOL, B, B), BF),
        ],
        in_specs=[SM, SM, HBM],
        out_specs=[SM, VM],
        scratch_shapes=[pltpu.VMEM((2, B, B), BF), pltpu.SemaphoreType.DMA((3,))],
        compiler_params=pltpu.CompilerParams(vmem_limit_bytes=4 << 20),
        cost_estimate=NOTHING,
        name="prepare",
    )(cols_t, outcols_t, in_hbm(vals))


CALLS = {
    "first": (1, {(2, 0): (0, 0), (1, 1): (0, 2), (2, 1): (1, 0), (3, 0): (1, 2)}, (4, 4)),
    "rest": (1, {(1, 0): (0, 0), (3, 1): (1, 0), (0, 0): (2, 0), (0, 1): (3, 0)}, (2,) * 4),
    "second": (
        2,
        {
            **{(2, 0): (0, 0), (1, 1): (1, 0), (2, 1): (2, 0), (3, 0): (3, 0)},
            **{(1, 0): (4, 0), (3, 1): (5, 0), (0, 0): (6, 0), (0, 1): (7, 0)},
        },
        (2,) * 8,
    ),
}


def product_kernel(call, table, pool_in, listing, *rest):
    chunk, targets, sizes = CALLS[call]
    n_halo = {"first": 1, "rest": 0, "second": 2}[call]
    halo, rest = rest[:n_halo], rest[n_halo:]
    outs, (pool, lines, away, right, twice, sem) = rest[: len(sizes)], rest[len(sizes) :]
    layer, _ = here()
    first_rows = A_PARTS[0] * B
    listed = pltpu.make_async_copy(listing.at[pl.ds(first_rows, 16)], lines, sem.at[0])
    listed.start()
    pieces = []
    if call == "first":
        pieces = [(halo[0], pool.at[B0 : B0 + B_PARTS[0]])]
        pieces += [(listing.at[pl.ds(p * B, B)], pool.at[A0 + p]) for p in range(A_PARTS[0])]
    elif call == "second":
        a_at, b_at = A0 + A_PARTS[0], B0 + B_PARTS[0]
        pieces = [(halo[0], pool.at[b_at : b_at + B_PARTS[1]])]
        pieces += [(halo[1], pool.at[a_at : a_at + A_PARTS[1]])]
    copies = [
        pltpu.make_async_copy(ref, dst, sem.at[1 + x]) for x, (ref, dst) in enumerate(pieces)
    ]
    for copy in copies:
        copy.start()
    listed.wait()
    away[...] = lines[:, :128].astype(F32).astype(I32)

    def row_of(above, r):
        return r + 2 * (chunk - 1) if above else -1 - r - 2 * (chunk - 1)

    def below_row(r, carry):
        i = row_of(0, r)

        def left(t):
            return table[LEFT + (i + 4) * 4 + t]

        def store(at, value):
            twice[at] = value

        for shift, above in targets:
            if not above:
                far = away[(i + 4) * 4 + ((layer + shift) & 3), 0]
                row_entries(i, far, layer, table, left, right, store, r * 4 + shift)
        return carry

    lax.fori_loop(0, 2, below_row, 0)
    for copy in copies:
        copy.wait()

    def compute(above, r, carry):
        i = row_of(above, r)
        lefts = [table[LEFT + (i + 4) * 4 + t] for t in range(4)]
        for shift in (2, 1, 3, 0):
            if (shift, above) not in targets:
                continue
            o = (layer + shift) & 3
            acc = jnp.zeros((B, B), F32)
            for t in range(4):
                at = (i * 4 + o) * 4 + t if above else (r * 4 + shift) * 4 + t
                place = table[at] if above else right[at]
                acc += lax.dot_general(
                    pool[lefts[t]],
                    pool[place],
                    (((1,), (1,)), ((), ())),
                    preferred_element_type=F32,
                )
            own = table[TWICE + i * 4 + o] if above else twice[r * 4 + shift]
            factor = jnp.where(own < ZERO, 2.0, 0.0).astype(F32)
            out, start = targets[shift, above]
            outs[out][start + r] = (factor * pool[own].astype(F32) - acc).astype(BF)
        return carry

    lax.fori_loop(0, 2, functools.partial(compute, 0), 0)
    lax.fori_loop(0, 2, functools.partial(compute, 1), 0)


def products(table, pool, halo, call):
    sizes = CALLS[call][2]
    return pl.pallas_call(
        functools.partial(product_kernel, call),
        out_shape=[jax.ShapeDtypeStruct((n, B, B), BF) for n in (*sizes, POOL)],
        in_specs=[SM, VM] + [ANY] * len(halo),
        out_specs=[VM] * (len(sizes) + 1),
        scratch_shapes=[
            pltpu.VMEM((16, B), BF),
            pltpu.VMEM((16, 128), I32),
            pltpu.SMEM((32,), I32),
            pltpu.SMEM((8,), I32),
            pltpu.SemaphoreType.DMA((2 + A_PARTS[0],)),
        ],
        input_output_aliases={1: len(sizes)},
        compiler_params=pltpu.CompilerParams(vmem_limit_bytes=4 << 20),
        cost_estimate=NOTHING,
        name=f"products_{call}",
    )(table, pool, *halo)


def total(*parts):
    return sum(part.astype(F32) for part in parts).astype(BF)


def add_kernel(*refs):
    parts, out = refs[:-1], refs[-1]
    out[...] = total(*[part[...] for part in parts])


def add(parts, name):
    return pl.pallas_call(
        add_kernel,
        out_shape=jax.ShapeDtypeStruct((2, B, B), BF),
        in_specs=[VM] * len(parts),
        out_specs=VM,
        compiler_params=pltpu.CompilerParams(vmem_limit_bytes=4 << 20),
        cost_estimate=NOTHING,
        name=name,
    )(*parts)


def adds_kernel(a, b, c, d, x, y):
    x[...] = total(a[...], b[:2])
    y[...] = total(c[...], d[:2])


def adds(a, b, c, d, name, cost):
    return pl.pallas_call(
        adds_kernel,
        out_shape=[jax.ShapeDtypeStruct((2, B, B), BF)] * 2,
        in_specs=[VM] * 4,
        out_specs=[VM] * 2,
        compiler_params=pltpu.CompilerParams(vmem_limit_bytes=4 << 20),
        cost_estimate=pl.CostEstimate(flops=0, bytes_accessed=cost, transcendentals=0),
        name=name,
    )(a, b, c, d)


def finish_kernel(sums, copied, *rest):
    n_in = 3 * len(sums) + len(copied)
    parts, (out, block, sem) = rest[:n_in], rest[-3:]
    copies = []

    def send(src, row):
        copy = pltpu.make_async_copy(src, out.at[row], sem.at[len(copies)])
        copy.start()
        copies.append(copy)

    for x, rows in enumerate(copied):
        for r in range(2):
            send(parts[3 * len(sums) + x].at[r], rows[r])
    for x, rows in enumerate(sums):
        own, plus, minus = parts[3 * x : 3 * x + 3]
        for r in range(2):
            block[2 * x + r] = total(own[r], plus[plus.shape[0] - 2 + r], minus[r])
            send(block.at[2 * x + r], rows[r])
    for copy in copies:
        copy.wait()


def finish(sums, copied, parts, before, name):
    n = 2 * len(sums) + 2 * len(copied)
    return pl.pallas_call(
        functools.partial(finish_kernel, sums, copied),
        out_shape=jax.ShapeDtypeStruct((8, B, B), BF),
        in_specs=[VM] * len(parts) + [HBM] * len(before),
        out_specs=HBM,
        scratch_shapes=[
            pltpu.VMEM((max(2 * len(sums), 1), B, B), BF),
            pltpu.SemaphoreType.DMA((n,)),
        ],
        input_output_aliases={len(parts): 0} if before else {},
        compiler_params=pltpu.CompilerParams(vmem_limit_bytes=4 << 20),
        cost_estimate=NOTHING,
        name=name,
    )(*parts, *before)


def per_device(cols, vals, outcols):
    both = lax.optimization_barrier
    a1, b1, a2, b2 = pack(cols.T, outcols.T, vals)
    a1 = shifted(a1, ROWS, 1)
    b1 = shifted(b1, ROWS, -1, False)
    a2 = shifted(a2, ROWS, 1)
    b2 = shifted(b2, ROWS, -1, False)
    table, pool = prepare(cols.T, outcols.T, vals)

    plus1, minus1, pool = products(table, pool, (a1, b1), "first")
    plus1, minus1 = shifted(plus1, "layer", 1), shifted(minus1, "layer", -1)
    up_b1, down1, own_b1, own1, pool = products(table, pool, (a1,), "rest")
    out2 = products(table, pool, (a1, b2, a2), "second")
    far_b2, up2, far2, down_b2, up_b2, down2, own_b2, own2, pool = out2
    (plus1, minus1), _ = both(((plus1, minus1), own_b2))
    far_b2 = shifted(far_b2, "layer", 1)
    down_b2 = shifted(down_b2, "layer", -1)
    far2 = shifted(far2, "layer", -1)
    up_b1, down1 = adds(up_b1, plus1, down1, minus1, "adds1", 40 << 20)
    up_b1 = shifted(up_b1, "layer", 1)
    down1 = shifted(down1, "layer", -1)
    up_b2 = shifted(add((up_b2, far_b2), "add_below2"), "layer", 1)
    up2 = shifted(up2, "layer", 1)
    down2 = shifted(add((down2, far2), "add2"), "layer", -1)
    below1 = shifted(total(own_b1, minus1[2:], up_b1), ROWS, -1)
    below2 = shifted(add((own_b2, down_b2, up_b2), "below2"), ROWS, -1)
    mine = finish(((0, 1),), ((7, 6),), (own1, plus1, down1, below1), (), "finish1")
    mine = finish(((2, 3),), ((5, 4),), (own2, up2, down2, below2), (mine,), "finish2")
    return mine[:, None]


def solution(mesh):
    in_specs = (
        P(ROWS, "layer"),
        P(ROWS, "layer", None, None),
        P(ROWS, None),
    )
    out_specs = P(ROWS, "layer", None, None)
    return jax.shard_map(
        per_device, mesh=mesh, in_specs=in_specs, out_specs=out_specs, check_vma=False
    )
```

```python
import functools

import jax
import jax.numpy as jnp
from jax import lax
from jax.experimental import pallas as pl
from jax.experimental.pallas import tpu as pltpu
from jax.sharding import PartitionSpec as P

ROWS = ("row", "col")
B = 256
BF = jnp.bfloat16
F32 = jnp.float32
I32 = jnp.int32
SM = pl.BlockSpec(memory_space=pltpu.SMEM)
VM = pl.BlockSpec(memory_space=pltpu.VMEM)
ANY = pl.BlockSpec(memory_space=pl.ANY)
HBM = pl.BlockSpec(memory_space=pltpu.HBM)

A_PARTS = (7, 5)
B_PARTS = (7, 4)
A0 = 32
B0 = A0 + sum(A_PARTS)
TURN = B0 + sum(B_PARTS)
ZERO = TURN + 2
POOL = ZERO + 1
TWICE, LEFT, OWN, ENTRIES = 64, 80, 112, 144


def shifted(value, axis, by, wrap=True):
    n = lax.axis_size(axis)
    pairs = [(i, (i + by) % n) for i in range(n) if wrap or 0 <= i + by < n]
    return lax.ppermute(value, axis, pairs)


def in_hbm(value):
    return pltpu.with_memory_space_constraint(value, pltpu.HBM)


def here():
    layer = lax.axis_index("layer").astype(I32)
    device = lax.axis_index(ROWS).astype(I32)
    return layer, device


def first_col(row, layer):
    return row - 6 + ((layer - row + 6) & 3)


def b_first(layer):
    return jnp.where(layer < 2, layer + 4, layer)


def a_count(m, layer):
    return 3 + jnp.where(m == ((layer + 2) & 3), 1, 0) - jnp.where(m == layer, 1, 0)


def a_start(m, layer):
    start = jnp.int32(0)
    for above in (3, 2, 1):
        start += jnp.where(m < above, a_count(above, layer), 0)
    return start


def b_turned(layer):
    return layer + jnp.where(layer < 2, 0, b_first(layer) - 1)


def slot_of(cols_t, row, col):
    hit = jnp.int32(-1)
    empty = jnp.int32(0)
    for s in range(4):
        c = cols_t[s, row]
        hit = jnp.where(c == col, s, hit)
        empty = jnp.where(c < 0, s, empty)
    return jnp.where(hit >= 0, hit, empty)


def pack_kernel(cols_hbm, outcols_hbm, vals, *rest):
    outs, (cols_t, outcols_t, sems, ints_sem) = rest[:4], rest[4:]
    ints = [
        pltpu.make_async_copy(cols_hbm, cols_t, ints_sem.at[0]),
        pltpu.make_async_copy(outcols_hbm, outcols_t, ints_sem.at[1]),
    ]
    for copy in ints:
        copy.start()
    for copy in ints:
        copy.wait()
    layer, device = here()
    base = device * 8
    copies = []

    def send(row, col, dst):
        slot = slot_of(cols_t, row, base + col)
        copy = pltpu.make_async_copy(vals.at[row, slot], dst, sems.at[len(copies)])
        copy.start()
        copies.append(copy)

    def a_block(p):
        m = jnp.int32(3)
        t = jnp.int32(p)
        for above in (3, 2, 1):
            past = p >= a_start(above - 1, layer)
            m = jnp.where(past, above - 1, m)
        t = p - a_start(m, layer)
        row = 4 + m
        return row, first_col(row, layer) + 4 * t

    def b_block(p):
        q = p + jnp.where(p >= b_turned(layer), 1, 0)
        k1 = b_first(layer)
        low = q < k1 - 1
        d = jnp.where(low, q, jnp.minimum(q - (k1 - 1), k1 + 2))
        return d, jnp.where(low, k1, k1 + 4) - 8

    p_a = p_b = 0
    for part in range(2):
        for p in range(A_PARTS[part]):
            dst = outs[0].at[pl.ds(p * B, B)] if part == 0 else outs[2].at[p]
            send(*a_block(p_a), dst)
            p_a += 1
        for p in range(B_PARTS[part]):
            send(*b_block(p_b), outs[2 * part + 1].at[p])
            p_b += 1
    line = lax.broadcasted_iota(I32, (16, B), 0)
    listing = jnp.zeros((16, B), F32)
    for m in range(4):
        for o in range(4):
            col = outcols_t[o, 4 + m]
            away = jnp.where(col >= 0, col - base - 4 - m, -1).astype(F32)
            listing = jnp.where(line == m * 4 + o, away, listing)
    outs[0][pl.ds(A_PARTS[0] * B, 16)] = listing.astype(BF)
    for copy in copies:
        copy.wait()


NOTHING = pl.CostEstimate(flops=0, bytes_accessed=0, transcendentals=0)


def pack(cols_t, outcols_t, vals):
    sizes = (A_PARTS[0], B_PARTS[0], A_PARTS[1], B_PARTS[1])
    shapes = [(A_PARTS[0] * B + 16, B)] + [(n, B, B) for n in sizes[1:]]
    return pl.pallas_call(
        pack_kernel,
        out_shape=[jax.ShapeDtypeStruct(shape, BF) for shape in shapes],
        in_specs=[HBM, HBM, HBM],
        out_specs=[VM] * 4,
        scratch_shapes=[
            pltpu.SMEM((4, 8), I32),
            pltpu.SMEM((4, 8), I32),
            pltpu.SemaphoreType.DMA((sum(sizes),)),
            pltpu.SemaphoreType.DMA((2,)),
        ],
        compiler_params=pltpu.CompilerParams(vmem_limit_bytes=4 << 20),
        cost_estimate=NOTHING,
        name="pack",
    )(in_hbm(cols_t), in_hbm(outcols_t), in_hbm(vals))


def left_place(i, t, layer):
    m = i + 4
    place = jnp.where((m == layer) & (t == 2), TURN, A0 + a_start(m, layer) + t)
    return jnp.where(first_col(i, layer) + 4 * t <= i + 6, place, ZERO)


def row_entries(i, away, layer, table, left, right, twice, at):
    first = first_col(i, layer)
    listed = away >= 0
    j = i + jnp.clip(away, 0, 12)
    first_j = first_col(j, layer)
    start_j = A0 + a_start(j + 4, layer)
    k1 = b_first(layer)
    gap = b_turned(layer)
    for t in range(4):
        k = first + 4 * t
        t_j = jnp.clip((k - first_j) >> 2, 0, 3)
        in_a = jnp.where((j + 4 == layer) & (t_j == 2), TURN, start_j + t_j)
        pos = j - 8 + jnp.where(k == k1, 0, k1 - 1)
        in_b = jnp.where(pos == gap, TURN + 1, B0 + pos - jnp.where(pos > gap, 1, 0))
        place = jnp.where(j < 0, in_a, table[OWN + jnp.clip(j, 0, 7) * 4 + t_j])
        place = jnp.clip(jnp.where(j < 8, place, in_b), 0, ZERO)
        ok = listed & (k >= j - 6) & (k <= i + 6)
        right[at * 4 + t] = jnp.where(ok, place, ZERO)
    doubled = listed & ((j & 3) == layer) & (j <= i + 6)
    t_i = jnp.clip((j - first) >> 2, 0, 3)
    twice(at, jnp.where(doubled, left(t_i), ZERO))


def prepare_kernel(cols_t, outcols_t, vals, table, pool, blocks, sem):
    layer, device = here()
    base = device * 8
    copies = [pltpu.make_async_copy(vals.reshape(32, B, B), pool.at[:A0], sem.at[2])]
    for x, (row, col) in enumerate(((layer, layer - 4), (4 + layer, 8 + layer))):
        slot = slot_of(cols_t, row, base + col)
        copies.append(pltpu.make_async_copy(vals.at[row, slot], blocks.at[x], sem.at[x]))
    for copy in copies:
        copy.start()
    pool[ZERO] = jnp.zeros((B, B), BF)

    def own_row(row, carry):
        first = first_col(row, layer)
        for t in range(4):
            place = row * 4 + slot_of(cols_t, row, base + first + 4 * t)
            table[OWN + row * 4 + t] = place
            valid = first + 4 * t <= row + 6

            @pl.when(row < 4)
            def _():
                table[LEFT + 16 + row * 4 + t] = jnp.where(valid, place, ZERO)
                table[LEFT + row * 4 + t] = left_place(row - 4, jnp.int32(t), layer)

        return carry

    lax.fori_loop(0, 8, own_row, 0)

    def one_row(i, carry):
        def left(t):
            return table[LEFT + 16 + i * 4 + t]

        def twice(at, value):
            table[TWICE + at] = value

        for o in range(4):
            col = outcols_t[o, i]
            away = jnp.where(col >= 0, col - base - i, -1)
            row_entries(i, away, layer, table, left, table, twice, i * 4 + o)
        return carry

    lax.fori_loop(0, 4, one_row, 0)
    for copy in copies:
        copy.wait()
    for x in range(2):
        pool[TURN + x] = blocks[x].T


def prepare(cols_t, outcols_t, vals):
    return pl.pallas_call(
        prepare_kernel,
        out_shape=[
            jax.ShapeDtypeStruct((ENTRIES,), I32),
            jax.ShapeDtypeStruct((POOL, B, B), BF),
        ],
        in_specs=[SM, SM, HBM],
        out_specs=[SM, VM],
        scratch_shapes=[pltpu.VMEM((2, B, B), BF), pltpu.SemaphoreType.DMA((3,))],
        compiler_params=pltpu.CompilerParams(vmem_limit_bytes=4 << 20),
        cost_estimate=NOTHING,
        name="prepare",
    )(cols_t, outcols_t, in_hbm(vals))


CALLS = {
    "first": (1, {(2, 0): (0, 0), (1, 1): (0, 2), (2, 1): (1, 0), (3, 0): (1, 2)}, (4, 4)),
    "rest": (1, {(1, 0): (0, 0), (3, 1): (1, 0), (0, 0): (2, 0), (0, 1): (3, 0)}, (2,) * 4),
    "second": (2, {(2, 0): (0, 0), (2, 1): (1, 0), (3, 0): (2, 0)}, (2,) * 3),
    "last": (
        2,
        {(1, 0): (0, 0), (1, 1): (1, 0), (3, 1): (2, 0), (0, 0): (3, 0), (0, 1): (4, 0)},
        (2,) * 5,
    ),
}


def product_kernel(call, table, pool_in, listing, *rest):
    chunk, targets, sizes = CALLS[call]
    n_halo = {"first": 1, "second": 2}.get(call, 0)
    halo, rest = rest[:n_halo], rest[n_halo:]
    outs, (pool, lines, away, right, twice, sem) = rest[: len(sizes)], rest[len(sizes) :]
    layer, _ = here()
    first_rows = A_PARTS[0] * B
    listed = pltpu.make_async_copy(listing.at[pl.ds(first_rows, 16)], lines, sem.at[0])
    listed.start()
    pieces = []
    if call == "first":
        pieces = [(halo[0], pool.at[B0 : B0 + B_PARTS[0]])]
        flat = pool.reshape(POOL * B, B)
        pieces += [(listing.at[pl.ds(0, first_rows)], flat.at[pl.ds(A0 * B, first_rows)])]
    elif call == "second":
        a_at, b_at = A0 + A_PARTS[0], B0 + B_PARTS[0]
        pieces = [(halo[0], pool.at[b_at : b_at + B_PARTS[1]])]
        pieces += [(halo[1], pool.at[a_at : a_at + A_PARTS[1]])]
    copies = [
        pltpu.make_async_copy(ref, dst, sem.at[1 + x]) for x, (ref, dst) in enumerate(pieces)
    ]
    for copy in copies:
        copy.start()
    listed.wait()
    away[...] = lines[:, :128].astype(F32).astype(I32)

    def row_of(above, r):
        return r + 2 * (chunk - 1) if above else r - 2 * chunk

    def below_row(r, carry):
        i = row_of(0, r)

        def left(t):
            return table[LEFT + (i + 4) * 4 + t]

        def store(at, value):
            twice[at] = value

        for shift, above in targets:
            if not above:
                far = away[(i + 4) * 4 + ((layer + shift) & 3), 0]
                row_entries(i, far, layer, table, left, right, store, r * 4 + shift)
        return carry

    lax.fori_loop(0, 2, below_row, 0)

    def compute(above, r, carry):
        i = row_of(above, r)
        lefts = [table[LEFT + (i + 4) * 4 + t] for t in range(4)]
        for shift in (2, 1, 3, 0):
            if (shift, above) not in targets:
                continue
            o = (layer + shift) & 3
            acc = jnp.zeros((B, B), F32)
            for t in range(4):
                at = (i * 4 + o) * 4 + t if above else (r * 4 + shift) * 4 + t
                place = table[at] if above else right[at]
                acc += lax.dot_general(
                    pool[lefts[t]],
                    pool[place],
                    (((1,), (1,)), ((), ())),
                    preferred_element_type=F32,
                )
            own = table[TWICE + i * 4 + o] if above else twice[r * 4 + shift]
            factor = jnp.where(own < ZERO, 2.0, 0.0).astype(F32)
            out, start = targets[shift, above]
            outs[out][start + r] = (factor * pool[own].astype(F32) - acc).astype(BF)
        return carry

    n_b = min(n_halo, 1)
    for copy in copies[:n_b]:
        copy.wait()
    lax.fori_loop(0, 2, functools.partial(compute, 1), 0)
    for copy in copies[n_b:]:
        copy.wait()
    lax.fori_loop(0, 2, functools.partial(compute, 0), 0)


def products(table, pool, halo, call):
    sizes = CALLS[call][2]
    return pl.pallas_call(
        functools.partial(product_kernel, call),
        out_shape=[jax.ShapeDtypeStruct((n, B, B), BF) for n in (*sizes, POOL)],
        in_specs=[SM, VM] + [ANY] * len(halo),
        out_specs=[VM] * (len(sizes) + 1),
        scratch_shapes=[
            pltpu.VMEM((16, B), BF),
            pltpu.VMEM((16, 128), I32),
            pltpu.SMEM((32,), I32),
            pltpu.SMEM((8,), I32),
            pltpu.SemaphoreType.DMA((3,)),
        ],
        input_output_aliases={1: len(sizes)},
        compiler_params=pltpu.CompilerParams(vmem_limit_bytes=4 << 20),
        cost_estimate=NOTHING,
        name=f"products_{call}",
    )(table, pool, *halo)


def total(*parts):
    return sum(part.astype(F32) for part in parts).astype(BF)


def add_kernel(*refs):
    parts, out = refs[:-1], refs[-1]
    out[...] = total(*[part[...] for part in parts])


def add(parts, name):
    return pl.pallas_call(
        add_kernel,
        out_shape=jax.ShapeDtypeStruct((2, B, B), BF),
        in_specs=[VM] * len(parts),
        out_specs=VM,
        compiler_params=pltpu.CompilerParams(vmem_limit_bytes=4 << 20),
        cost_estimate=NOTHING,
        name=name,
    )(*parts)


def adds_kernel(a, b, c, d, x, y):
    x[...] = total(a[...], b[:2])
    y[...] = total(c[...], d[:2])


def adds(a, b, c, d, name, cost):
    return pl.pallas_call(
        adds_kernel,
        out_shape=[jax.ShapeDtypeStruct((2, B, B), BF)] * 2,
        in_specs=[VM] * 4,
        out_specs=[VM] * 2,
        compiler_params=pltpu.CompilerParams(vmem_limit_bytes=4 << 20),
        cost_estimate=pl.CostEstimate(flops=0, bytes_accessed=cost, transcendentals=0),
        name=name,
    )(a, b, c, d)


def finish_kernel(row, below_row, own, plus, minus, below, *rest):
    out, block, sem = rest[-3:]
    whole = pltpu.make_async_copy(below, out.at[below_row : below_row + 2], sem.at[0])
    whole.start()
    block[...] = total(own[...], plus[plus.shape[0] - 2 :], minus[...])
    summed = pltpu.make_async_copy(block, out.at[row : row + 2], sem.at[1])
    summed.start()
    whole.wait()
    summed.wait()


def finish(row, below_row, parts, before, name):
    return pl.pallas_call(
        functools.partial(finish_kernel, row, below_row),
        out_shape=jax.ShapeDtypeStruct((8, B, B), BF),
        in_specs=[VM] * len(parts) + [HBM] * len(before),
        out_specs=HBM,
        scratch_shapes=[pltpu.VMEM((2, B, B), BF), pltpu.SemaphoreType.DMA((2,))],
        input_output_aliases={len(parts): 0} if before else {},
        compiler_params=pltpu.CompilerParams(vmem_limit_bytes=4 << 20),
        cost_estimate=NOTHING,
        name=name,
    )(*parts, *before)


def per_device(cols, vals, outcols):
    both = lax.optimization_barrier
    a1, b1, a2, b2 = pack(cols.T, outcols.T, vals)
    a1 = shifted(a1, ROWS, 1)
    b1 = shifted(b1, ROWS, -1, False)
    a2 = shifted(a2, ROWS, 1)
    b2 = shifted(b2, ROWS, -1, False)
    table, pool = prepare(cols.T, outcols.T, vals)

    plus1, minus1, pool = products(table, pool, (a1, b1), "first")
    plus1, minus1 = shifted(plus1, "layer", 1), shifted(minus1, "layer", -1)
    up_b1, down1, own_b1, own1, pool = products(table, pool, (a1,), "rest")
    far_b2, far2, down_b2, pool = products(table, pool, (a1, b2, a2), "second")
    up_b2, up2, down2, own_b2, own2, pool = products(table, pool, (a1,), "last")
    (plus1, minus1), _ = both(((plus1, minus1), down_b2))
    far_b2 = shifted(far_b2, "layer", 1)
    down_b2 = shifted(down_b2, "layer", -1)
    far2 = shifted(far2, "layer", -1)
    up_b1, down1 = adds(up_b1, plus1, down1, minus1, "adds1", 40 << 20)
    up_b1 = shifted(up_b1, "layer", 1)
    down1 = shifted(down1, "layer", -1)
    up_b2 = shifted(add((up_b2, far_b2), "add_below2"), "layer", 1)
    up2 = shifted(up2, "layer", 1)
    down2 = shifted(add((down2, far2), "add2"), "layer", -1)
    below1 = shifted(total(own_b1, minus1[2:], up_b1), ROWS, -1)
    below2 = shifted(add((own_b2, down_b2, up_b2), "below2"), ROWS, -1)
    mine = finish(0, 6, (own1, plus1, down1, below1), (), "finish1")
    mine = finish(2, 4, (own2, up2, down2, below2), (mine,), "finish2")
    return mine[:, None]


def solution(mesh):
    in_specs = (
        P(ROWS, "layer"),
        P(ROWS, "layer", None, None),
        P(ROWS, None),
    )
    out_specs = P(ROWS, "layer", None, None)
    return jax.shard_map(
        per_device, mesh=mesh, in_specs=in_specs, out_specs=out_specs, check_vma=False
    )
```
